32 devices in a mesh: dp: 4 (over z), blk: 4 (over x, core), ulysses: 2 (over y).
Axes of the slice: x: 2, y: 2, z: 4, core: 2. Of those that a mesh axis runs over, the one named last changes fastest.
Arguments:
- block_input: bfloat16 [8, 512, 2048], P('dp', ('blk', 'ulysses')), may hold values from -6 to 6
- positions: int32 [8, 512], P('dp'), may hold values from 0 to 511, as said below
- cotangent: bfloat16 [8, 512, 2048], P('dp', ('blk', 'ulysses')), may hold values from -6 to 6
- norm_gains: bfloat16 [2, 2048], P(None, ('dp', 'blk', 'ulysses')), may hold values from 0.099609375 to 1.8984375
- head_gains: bfloat16 [256], P(('dp', 'blk', 'ulysses')), may hold values from 0.099609375 to 1.8984375
- w_query: bfloat16 [2048, 2048], P(('dp', 'blk', 'ulysses')), may hold values from -0.125 to 0.125
- w_key: bfloat16 [2048, 1024], P(('dp', 'blk', 'ulysses')), may hold values from -0.125 to 0.125
- w_value: bfloat16 [2048, 1024], P(('dp', 'blk', 'ulysses')), may hold values from -0.125 to 0.125
- w_out: bfloat16 [2048, 2048], P(('dp', 'blk', 'ulysses')), may hold values from -0.75 to 0.75
- w_gate: bfloat16 [2048, 6144], P(None, ('dp', 'blk', 'ulysses')), may hold values from -0.125 to 0.125
- w_up: bfloat16 [2048, 6144], P(None, ('dp', 'blk', 'ulysses')), may hold values from -0.125 to 0.125
- w_down: bfloat16 [6144, 2048], P(('dp', 'blk', 'ulysses')), may hold values from -0.078125 to 0.078125
Outputs:
- block_output: bfloat16 [8, 512, 2048], P('dp', ('blk', 'ulysses'))
- grad_input: float32 [8, 512, 2048], P('dp', ('blk', 'ulysses'))
- grad_norm_gains: float32 [2, 2048], P(None, ('dp', 'blk', 'ulysses'))
- grad_head_gains: float32 [256], P(('dp', 'blk', 'ulysses'))
- grad_w_query: float32 [2048, 2048], P(('dp', 'blk', 'ulysses'))
- grad_w_key: float32 [2048, 1024], P(('dp', 'blk', 'ulysses'))
- grad_w_value: float32 [2048, 1024], P(('dp', 'blk', 'ulysses'))
- grad_w_out: float32 [2048, 2048], P(('dp', 'blk', 'ulysses'))
- grad_w_gate: float32 [2048, 6144], P(None, ('dp', 'blk', 'ulysses'))
- grad_w_up: float32 [2048, 6144], P(None, ('dp', 'blk', 'ulysses'))
- grad_w_down: float32 [6144, 2048], P(('dp', 'blk', 'ulysses'))
The draws below stay inside these ranges and needn't reach their ends.
Inputs may be any that keep to these rules, and one draw needn't show every extreme that they name: Each row of positions holds every position of 0 to 511 once, in runs of 32 ascending consecutive positions that start at multiples of 32; the order of the runs is drawn for each sequence.
All inputs are finite; a program needn't handle non-finite values.
Results may differ from the reference program's by a relative error of at most 0.02.
Values may be sent and summed in bfloat16 or wider, within the bound.
No kernel may reach another device: no remote copies, remote signals or barrier semaphores. Data moves between devices by JAX's collectives and lax.ppermute only.
A program may use at most 448 MiB of HBM per device.

```python
import math
import jax
import jax.numpy as jnp
from jax import lax

D = 2048
QH = 16
KH = 8
HD = 128
FF = 6144
BLOCK_TOK = 64
LENGTH = 512
BATCH = 8


def draw_positions(key, part):
    half_block = BLOCK_TOK // 2
    block_count = LENGTH // half_block
    row_keys = jax.random.split(key, BATCH)
    orders = jax.vmap(lambda row_key: jax.random.permutation(row_key, block_count))(row_keys)
    within = jnp.arange(half_block, dtype=jnp.int32)
    return (orders.astype(jnp.int32)[:, :, None] * half_block + within[None, None, :]).reshape(BATCH, LENGTH)


def spiked(values, rng, source, target, shards_of, factor):
    owner, partner = [(jnp.arange(values.shape[position]) // (values.shape[position] // shards_of)).reshape([-1 if axis == position else 1 for axis in range(values.ndim)]) for position in (source, target)]
    chosen = jax.random.permutation(rng, shards_of)[partner]
    strong = (owner == chosen) | (owner == (partner + shards_of // 2) % shards_of)
    return jnp.where(strong, factor * values, values)


def shard_levels(stream_key, extent, pieces, least, largest):
    def one(position, parts):
        draws = jax.random.uniform(jax.random.fold_in(jax.random.fold_in(stream_key, 6), position), (parts,), jnp.float32, least / len(pieces), largest / len(pieces))
        return jnp.repeat(jnp.exp(draws), extent[position] // parts).reshape((-1,) + (1,) * (len(extent) - position - 1))

    loudness = one(*pieces[0])
    for cut in pieces[1:]:
        loudness = loudness * one(*cut)
    return loudness


def centred(key, extent, spread, reach, cuts=(), kind=jnp.bfloat16):
    level = shard_levels(key, extent, cuts, -0.22, 0.18) if cuts else 1.0
    entries = jax.random.normal(key, extent, jnp.float32) * spread * level
    return jnp.minimum(jnp.maximum(entries, -reach), reach).astype(kind)


def heavy_noise(own_key, extent, spread, limit, pieces, heavy, kind=jnp.bfloat16):
    result = spread * jax.random.normal(own_key, extent, jnp.float32)
    if pieces:
        result = result * shard_levels(own_key, extent, pieces, -0.22, 0.18)
    return jnp.clip(spiked(result, jax.random.fold_in(own_key, 3), *heavy), -limit, limit).astype(kind)


def setup_inputs(seed: int = 0) -> dict:
    arg_keys = jax.random.split(jax.random.key(seed), 13)
    block_input = heavy_noise(arg_keys[0], (BATCH, LENGTH, D), 1.0, 6.0, ((0, 4), (1, 8)), (1, 2, 8, 2.0))
    positions = draw_positions(jax.random.fold_in(arg_keys[12], 71), 0)
    cotangent = centred(arg_keys[2], (BATCH, LENGTH, D), 1.0, 6.0, ((0, 4), (1, 8)))
    norm_gains = jnp.clip(1.0 + 0.18 * jax.random.normal(arg_keys[3], (2, D), jnp.float32), 0.099609375, 1.8984375).astype(jnp.bfloat16)
    head_gains = jnp.clip(1.0 + 0.18 * jax.random.normal(arg_keys[4], (2 * HD,), jnp.float32), 0.099609375, 1.8984375).astype(jnp.bfloat16)
    w_query = centred(arg_keys[5], (D, QH * HD), D ** -0.5, 0.125, ((0, 32),))
    w_key = centred(arg_keys[6], (D, KH * HD), D ** -0.5, 0.125, ((0, 32),))
    w_value = centred(arg_keys[7], (D, KH * HD), D ** -0.5, 0.125, ((0, 32),))
    w_out = centred(arg_keys[8], (QH * HD, D), (max(1, QH * HD * 16 // LENGTH)) ** -0.5, 0.75, ((0, 32),))
    w_gate = centred(arg_keys[9], (D, FF), D ** -0.5, 0.125, ((1, 32),))
    w_up = centred(arg_keys[10], (D, FF), D ** -0.5, 0.125, ((1, 32),))
    w_down = centred(arg_keys[11], (FF, D), FF ** -0.5, 0.078125, ((0, 32),))
    return dict(block_input=block_input, positions=positions, cotangent=cotangent, norm_gains=norm_gains, head_gains=head_gains, w_query=w_query, w_key=w_key, w_value=w_value, w_out=w_out, w_gate=w_gate, w_up=w_up, w_down=w_down)


norm_eps = 1e-06
rope_base = 1000000.0

def rms_scale(values):
    return lax.rsqrt(lax.optimization_barrier(jnp.mean(values * values, axis=-1, keepdims=True)) + norm_eps)

def rms_back(values, scale_rows, gain, grad_out, axes_summed):
    unit_rows = values * scale_rows
    scaled_grad = grad_out * gain
    grad_in = scale_rows * (scaled_grad - unit_rows * lax.optimization_barrier(jnp.mean(scaled_grad * unit_rows, axis=-1, keepdims=True)))
    return (grad_in, lax.optimization_barrier(jnp.sum(grad_out * unit_rows, axis=axes_summed)))

def rope_tables(where_rows, head_width):
    half_width = head_width // 2
    inverse = rope_base ** (-(jnp.arange(half_width, dtype=jnp.float32) * 2.0 / head_width))
    angles = where_rows.astype(jnp.float32)[:, None] * inverse[None, :]
    return (jnp.cos(angles)[:, None, :], jnp.sin(angles)[:, None, :])

def rotate(values, cos_table, sin_table):
    half_width = values.shape[-1] // 2
    first_half = values[..., :half_width]
    second_half = values[..., half_width:]
    return jnp.concatenate([first_half * cos_table - second_half * sin_table, second_half * cos_table + first_half * sin_table], axis=-1)

def unrotate(grads, cos_table, sin_table):
    half_width = grads.shape[-1] // 2
    first_half = grads[..., :half_width]
    second_half = grads[..., half_width:]
    return jnp.concatenate([first_half * cos_table + second_half * sin_table, second_half * cos_table - first_half * sin_table], axis=-1)

def attend(queries, key_rows, values, query_where, key_where):
    row_count, kv_heads, group_size, head_width = queries.shape
    block_rows = math.gcd(512, row_count)
    block_count = row_count // block_rows
    inv_root = 1.0 / math.sqrt(head_width)
    keys_float = key_rows.astype(jnp.float32)
    values_float = values.astype(jnp.float32)

    def one_block(inputs):
        query_block, block_where = inputs
        scores = jnp.einsum('qkgd,skd->kgqs', query_block.astype(jnp.float32), keys_float) * inv_root
        allowed = key_where[None, None, None, :] <= block_where[None, None, :, None]
        log_totals = jnp.log(lax.optimization_barrier(jnp.sum(jnp.where(allowed, jnp.exp(scores), 0.0), axis=-1)))
        weights = jnp.where(allowed, jnp.exp(scores - log_totals[..., None]), 0.0).astype(jnp.bfloat16)
        attended = jnp.einsum('kgqs,skd->qkgd', weights.astype(jnp.float32), values_float)
        return (attended.astype(jnp.bfloat16), log_totals)
    attended, log_totals = lax.map(one_block, (queries.reshape(block_count, block_rows, kv_heads, group_size, head_width), query_where.reshape(block_count, block_rows)))
    return (attended.reshape(row_count, kv_heads * group_size * head_width), log_totals)

def attend_back(queries, key_rows, values, query_where, key_where, attended, log_totals, grad_attended):
    row_count, kv_heads, group_size, head_width = queries.shape
    key_count = key_rows.shape[0]
    block_rows = math.gcd(512, row_count)
    block_count = row_count // block_rows
    inv_root = 1.0 / math.sqrt(head_width)
    keys_float = key_rows.astype(jnp.float32)
    values_float = values.astype(jnp.float32)
    deltas = lax.optimization_barrier(jnp.sum((grad_attended.astype(jnp.float32) * attended.astype(jnp.float32)).reshape(row_count, kv_heads, group_size, head_width), axis=-1))

    def one_block(running, inputs):
        key_grad, value_grad = running
        query_block, block_where, block_log, grad_block, block_delta = inputs
        query_float = query_block.astype(jnp.float32)
        grad_float = grad_block.astype(jnp.float32)
        scores = jnp.einsum('qkgd,skd->kgqs', query_float, keys_float) * inv_root
        allowed = key_where[None, None, None, :] <= block_where[None, None, :, None]
        weights = jnp.where(allowed, jnp.exp(scores - block_log[..., None]), 0.0)
        grad_weights = jnp.einsum('qkgd,skd->kgqs', grad_float, values_float)
        grad_scores = (weights * (grad_weights - jnp.moveaxis(block_delta, 0, 2)[..., None])).astype(jnp.bfloat16).astype(jnp.float32)
        query_grad = jnp.einsum('kgqs,skd->qkgd', grad_scores, keys_float) * inv_root
        key_grad = key_grad + jnp.einsum('kgqs,qkgd->skd', grad_scores, query_float) * inv_root
        weights_low = weights.astype(jnp.bfloat16).astype(jnp.float32)
        value_grad = value_grad + jnp.einsum('kgqs,qkgd->skd', weights_low, grad_float)
        return ((key_grad, value_grad), query_grad)
    initial = (jnp.zeros((key_count, kv_heads, head_width), jnp.float32), jnp.zeros((key_count, kv_heads, head_width), jnp.float32))
    inputs = (queries.reshape(block_count, block_rows, kv_heads, group_size, head_width), query_where.reshape(block_count, block_rows), log_totals, grad_attended.reshape(block_count, block_rows, kv_heads, group_size, head_width), deltas.reshape(block_count, block_rows, kv_heads, group_size))
    (key_grad, value_grad), query_grad = lax.scan(one_block, initial, inputs)
    return (query_grad.reshape(row_count, kv_heads * group_size * head_width), key_grad, value_grad)

def reference(block_input, positions, cotangent, norm_gains, head_gains, w_query, w_key, w_value, w_out, w_gate, w_up, w_down):
    gain_in = norm_gains[0].astype(jnp.float32)
    gain_mid = norm_gains[1].astype(jnp.float32)
    query_gain = head_gains[:HD].astype(jnp.float32)
    key_gain = head_gains[HD:].astype(jnp.float32)
    group_size = QH // KH

    def one_sequence(running, inputs):
        tokens, where_rows, cot_rows = inputs
        tokens_float = tokens.astype(jnp.float32)
        scale_in = rms_scale(tokens_float)
        normed_in = (tokens_float * scale_in * gain_in).astype(jnp.bfloat16)
        query_raw = jnp.dot(normed_in, w_query, preferred_element_type=jnp.float32).reshape(LENGTH, QH, HD)
        key_raw = jnp.dot(normed_in, w_key, preferred_element_type=jnp.float32).reshape(LENGTH, KH, HD)
        value_rows = jnp.dot(normed_in, w_value, preferred_element_type=jnp.float32).astype(jnp.bfloat16)
        query_scale = rms_scale(query_raw)
        key_scale = rms_scale(key_raw)
        cos_table, sin_table = rope_tables(where_rows, HD)
        query_rot = rotate(query_raw * query_scale * query_gain, cos_table, sin_table).astype(jnp.bfloat16)
        key_rot = rotate(key_raw * key_scale * key_gain, cos_table, sin_table).astype(jnp.bfloat16)
        query_groups = query_rot.reshape(LENGTH, KH, group_size, HD)
        value_heads = value_rows.reshape(LENGTH, KH, HD)
        attended, log_totals = attend(query_groups, key_rot, value_heads, where_rows, where_rows)
        middle = tokens_float + jnp.dot(attended, w_out, preferred_element_type=jnp.float32)
        scale_mid = rms_scale(middle)
        normed_mid = (middle * scale_mid * gain_mid).astype(jnp.bfloat16)
        gate_pre = jnp.dot(normed_mid, w_gate, preferred_element_type=jnp.float32)
        up_pre = jnp.dot(normed_mid, w_up, preferred_element_type=jnp.float32)
        gate_sigmoid = jax.nn.sigmoid(gate_pre)
        hidden = (gate_pre * gate_sigmoid * up_pre).astype(jnp.bfloat16)
        output_rows = (middle + jnp.dot(hidden, w_down, preferred_element_type=jnp.float32)).astype(jnp.bfloat16)
        grad_w_down = jnp.dot(hidden.T, cot_rows, preferred_element_type=jnp.float32)
        grad_hidden = jnp.dot(cot_rows, w_down.T, preferred_element_type=jnp.float32)
        grad_gate = (grad_hidden * up_pre * gate_sigmoid * (1.0 + gate_pre * (1.0 - gate_sigmoid))).astype(jnp.bfloat16)
        grad_upward = (grad_hidden * gate_pre * gate_sigmoid).astype(jnp.bfloat16)
        grad_w_gate = jnp.dot(normed_mid.T, grad_gate, preferred_element_type=jnp.float32)
        grad_w_up = jnp.dot(normed_mid.T, grad_upward, preferred_element_type=jnp.float32)
        grad_normed_mid = jnp.dot(grad_gate, w_gate.T, preferred_element_type=jnp.float32) + jnp.dot(grad_upward, w_up.T, preferred_element_type=jnp.float32)
        grad_mid_norm, grad_gain_mid = rms_back(middle, scale_mid, gain_mid, grad_normed_mid, 0)
        grad_middle = cot_rows.astype(jnp.float32) + grad_mid_norm
        grad_middle_low = grad_middle.astype(jnp.bfloat16)
        grad_w_out = jnp.dot(attended.T, grad_middle_low, preferred_element_type=jnp.float32)
        grad_attended = jnp.dot(grad_middle_low, w_out.T, preferred_element_type=jnp.float32).astype(jnp.bfloat16)
        query_grad, key_grad, value_grad = attend_back(query_groups, key_rot, value_heads, where_rows, where_rows, attended, log_totals, grad_attended)
        query_low = lax.optimization_barrier(query_grad.reshape(LENGTH, QH, HD).astype(jnp.bfloat16)).astype(jnp.float32)
        key_low = lax.optimization_barrier(key_grad.astype(jnp.bfloat16)).astype(jnp.float32)
        value_low = value_grad.reshape(LENGTH, KH * HD).astype(jnp.bfloat16)
        query_pre, grad_query_gain = rms_back(query_raw, query_scale, query_gain, unrotate(query_low, cos_table, sin_table), (0, 1))
        key_pre, grad_key_gain = rms_back(key_raw, key_scale, key_gain, unrotate(key_low, cos_table, sin_table), (0, 1))
        query_pre_low = query_pre.reshape(LENGTH, QH * HD).astype(jnp.bfloat16)
        key_pre_low = key_pre.reshape(LENGTH, KH * HD).astype(jnp.bfloat16)
        grad_w_query = jnp.dot(normed_in.T, query_pre_low, preferred_element_type=jnp.float32)
        grad_w_key = jnp.dot(normed_in.T, key_pre_low, preferred_element_type=jnp.float32)
        grad_w_value = jnp.dot(normed_in.T, value_low, preferred_element_type=jnp.float32)
        grad_normed_in = jnp.dot(query_pre_low, w_query.T, preferred_element_type=jnp.float32) + jnp.dot(key_pre_low, w_key.T, preferred_element_type=jnp.float32) + jnp.dot(value_low, w_value.T, preferred_element_type=jnp.float32)
        grad_in_norm, grad_gain_in = rms_back(tokens_float, scale_in, gain_in, grad_normed_in, 0)
        grad_rows = grad_middle + grad_in_norm
        terms = (grad_w_query, grad_w_key, grad_w_value, grad_w_out, grad_w_gate, grad_w_up, grad_w_down, grad_gain_in, grad_gain_mid, grad_query_gain, grad_key_gain)
        running = tuple((total + term for total, term in zip(running, terms)))
        return (running, (output_rows, grad_rows))
    initial = (jnp.zeros(w_query.shape, jnp.float32), jnp.zeros(w_key.shape, jnp.float32), jnp.zeros(w_value.shape, jnp.float32), jnp.zeros(w_out.shape, jnp.float32), jnp.zeros(w_gate.shape, jnp.float32), jnp.zeros(w_up.shape, jnp.float32), jnp.zeros(w_down.shape, jnp.float32), jnp.zeros((D,), jnp.float32), jnp.zeros((D,), jnp.float32), jnp.zeros((HD,), jnp.float32), jnp.zeros((HD,), jnp.float32))
    totals, (block_output, grad_input) = lax.scan(one_sequence, initial, (block_input, positions, cotangent))
    grad_norm_gains = jnp.stack([totals[7], totals[8]])
    grad_head_gains = jnp.concatenate([totals[9], totals[10]])
    return (block_output, grad_input, grad_norm_gains, grad_head_gains, totals[0], totals[1], totals[2], totals[3], totals[4], totals[5], totals[6])
```

```python
import math

import jax
import jax.numpy as jnp
from jax import lax
from jax.sharding import PartitionSpec as P

QH = 16
KH = 8
HD = 128

PLANE = ("blk", "ulysses")


norm_eps = 1e-06
rope_base = 1000000.0


def rms_scale(values):
    return lax.rsqrt(jnp.mean(values * values, axis=-1, keepdims=True) + norm_eps)


def rms_back(values, scale_rows, gain, grad_out, axes_summed):
    unit_rows = values * scale_rows
    scaled_grad = grad_out * gain
    grad_in = scale_rows * (
        scaled_grad - unit_rows * jnp.mean(scaled_grad * unit_rows, axis=-1, keepdims=True)
    )
    return (grad_in, jnp.sum(grad_out * unit_rows, axis=axes_summed))


def rope_tables(where_rows, head_width):
    half_width = head_width // 2
    inverse = rope_base ** (-(jnp.arange(half_width, dtype=jnp.float32) * 2.0 / head_width))
    angles = where_rows.astype(jnp.float32)[:, None] * inverse[None, :]
    return (jnp.cos(angles)[:, None, :], jnp.sin(angles)[:, None, :])


def rotate(values, cos_table, sin_table):
    half_width = values.shape[-1] // 2
    first_half = values[..., :half_width]
    second_half = values[..., half_width:]
    return jnp.concatenate(
        [
            first_half * cos_table - second_half * sin_table,
            second_half * cos_table + first_half * sin_table,
        ],
        axis=-1,
    )


def unrotate(grads, cos_table, sin_table):
    half_width = grads.shape[-1] // 2
    first_half = grads[..., :half_width]
    second_half = grads[..., half_width:]
    return jnp.concatenate(
        [
            first_half * cos_table + second_half * sin_table,
            second_half * cos_table - first_half * sin_table,
        ],
        axis=-1,
    )


def attend(queries, key_rows, values, query_where, key_where):
    row_count, kv_heads, group_size, head_width = queries.shape
    block_rows = math.gcd(512, row_count)
    block_count = row_count // block_rows
    inv_root = 1.0 / math.sqrt(head_width)

    def one_block(inputs):
        query_block, block_where = inputs
        scores = (
            jnp.einsum("qkgd,skd->kgqs", query_block, key_rows, preferred_element_type=jnp.float32)
            * inv_root
        )
        allowed = key_where[None, None, None, :] <= block_where[None, None, :, None]
        log_totals = jnp.log(jnp.sum(jnp.where(allowed, jnp.exp(scores), 0.0), axis=-1))
        weights = jnp.where(allowed, jnp.exp(scores - log_totals[..., None]), 0.0).astype(
            jnp.bfloat16
        )
        attended = jnp.einsum("kgqs,skd->qkgd", weights, values, preferred_element_type=jnp.float32)
        return (attended.astype(jnp.bfloat16), log_totals)

    attended, log_totals = lax.map(
        one_block,
        (
            queries.reshape(block_count, block_rows, kv_heads, group_size, head_width),
            query_where.reshape(block_count, block_rows),
        ),
    )
    return (attended.reshape(row_count, kv_heads * group_size * head_width), log_totals)


def attend_back(
    queries, key_rows, values, query_where, key_where, attended, log_totals, grad_attended
):
    row_count, kv_heads, group_size, head_width = queries.shape
    key_count = key_rows.shape[0]
    block_rows = math.gcd(512, row_count)
    block_count = row_count // block_rows
    inv_root = 1.0 / math.sqrt(head_width)
    deltas = jnp.sum(
        (grad_attended.astype(jnp.float32) * attended.astype(jnp.float32)).reshape(
            row_count, kv_heads, group_size, head_width
        ),
        axis=-1,
    )

    def one_block(running, inputs):
        key_grad, value_grad = running
        query_block, block_where, block_log, grad_block, block_delta = inputs
        scores = (
            jnp.einsum("qkgd,skd->kgqs", query_block, key_rows, preferred_element_type=jnp.float32)
            * inv_root
        )
        allowed = key_where[None, None, None, :] <= block_where[None, None, :, None]
        weights = jnp.where(allowed, jnp.exp(scores - block_log[..., None]), 0.0)
        grad_weights = jnp.einsum(
            "qkgd,skd->kgqs", grad_block, values, preferred_element_type=jnp.float32
        )
        grad_scores = (
            weights * (grad_weights - jnp.moveaxis(block_delta, 0, 2)[..., None])
        ).astype(jnp.bfloat16)
        query_grad = (
            jnp.einsum("kgqs,skd->qkgd", grad_scores, key_rows, preferred_element_type=jnp.float32)
            * inv_root
        )
        key_grad = (
            key_grad
            + jnp.einsum(
                "kgqs,qkgd->skd", grad_scores, query_block, preferred_element_type=jnp.float32
            )
            * inv_root
        )
        value_grad = value_grad + jnp.einsum(
            "kgqs,qkgd->skd",
            weights.astype(jnp.bfloat16),
            grad_block,
            preferred_element_type=jnp.float32,
        )
        return ((key_grad, value_grad), query_grad)

    initial = (
        jnp.zeros((key_count, kv_heads, head_width), jnp.float32),
        jnp.zeros((key_count, kv_heads, head_width), jnp.float32),
    )
    inputs = (
        queries.reshape(block_count, block_rows, kv_heads, group_size, head_width),
        query_where.reshape(block_count, block_rows),
        log_totals,
        grad_attended.reshape(block_count, block_rows, kv_heads, group_size, head_width),
        deltas.reshape(block_count, block_rows, kv_heads, group_size),
    )
    (key_grad, value_grad), query_grad = lax.scan(one_block, initial, inputs)
    return (
        query_grad.reshape(row_count, kv_heads * group_size * head_width),
        key_grad.reshape(key_count, kv_heads * head_width),
        value_grad.reshape(key_count, kv_heads * head_width),
    )


def fetch_attention(norm_gains, head_gains, w_query, w_key, w_value, w_out):
    return (
        lax.all_gather(w_query, ("dp", "blk", "ulysses"), axis=0, tiled=True),
        lax.all_gather(w_key, ("dp", "blk", "ulysses"), axis=0, tiled=True),
        lax.all_gather(w_value, ("dp", "blk", "ulysses"), axis=0, tiled=True),
        lax.all_gather(w_out, ("dp", "blk", "ulysses"), axis=0, tiled=True),
        lax.all_gather(norm_gains, ("dp", "blk", "ulysses"), axis=1, tiled=True),
        lax.all_gather(head_gains, ("dp", "blk", "ulysses"), axis=0, tiled=True),
    )


def sum_over_group(term_rows, local_rows):
    return lax.psum_scatter(
        term_rows(jnp.int32(0), lax.axis_size("ulysses") * local_rows),
        "ulysses",
        scatter_dimension=0,
        tiled=True,
    )


def ffn_forward(ffn_in, gate_weight, up_weight):
    gate_pre = jnp.dot(ffn_in, gate_weight, preferred_element_type=jnp.float32)
    up_pre = jnp.dot(ffn_in, up_weight, preferred_element_type=jnp.float32)
    gate_sigmoid = jax.nn.sigmoid(gate_pre)
    return (gate_pre, up_pre, gate_sigmoid, (gate_pre * gate_sigmoid * up_pre).astype(jnp.bfloat16))


def ffn_backward(grad_hidden, gate_pre, up_pre, gate_sigmoid):
    grad_gate = (
        grad_hidden * up_pre * gate_sigmoid * (1.0 + gate_pre * (1.0 - gate_sigmoid))
    ).astype(jnp.bfloat16)
    grad_upward = (grad_hidden * gate_pre * gate_sigmoid).astype(jnp.bfloat16)
    return (grad_gate, grad_upward)


def per_device(
    block_input,
    positions,
    cotangent,
    norm_gains,
    head_gains,
    w_query,
    w_key,
    w_value,
    w_out,
    w_gate,
    w_up,
    w_down,
):
    seq_count, block_tok, model_width = block_input.shape
    ulysses_size = lax.axis_size("ulysses")
    local_rows = seq_count * block_tok
    group_rows = ulysses_size * block_tok
    group_size = QH // KH
    local_kv = KH // ulysses_size
    my_block = lax.axis_index("blk") * ulysses_size + lax.axis_index("ulysses")
    where_rows = lax.dynamic_slice_in_dim(positions, my_block * block_tok, block_tok, 1).reshape(
        local_rows
    )
    group_where = lax.dynamic_slice_in_dim(
        positions, lax.axis_index("blk") * group_rows, group_rows, 1
    )
    full_query, full_key, full_value, full_out, full_gains, full_heads = fetch_attention(
        norm_gains, head_gains, w_query, w_key, w_value, w_out
    )
    gain_in = full_gains[0].astype(jnp.float32)
    gain_mid = full_gains[1].astype(jnp.float32)
    query_gain = full_heads[:HD].astype(jnp.float32)
    key_gain = full_heads[HD:].astype(jnp.float32)
    tokens_float = block_input.reshape(local_rows, model_width).astype(jnp.float32)
    scale_in = rms_scale(tokens_float)
    normed_in = (tokens_float * scale_in * gain_in).astype(jnp.bfloat16)
    query_raw = jnp.dot(normed_in, full_query, preferred_element_type=jnp.float32).reshape(
        local_rows, QH, HD
    )
    key_raw = jnp.dot(normed_in, full_key, preferred_element_type=jnp.float32).reshape(
        local_rows, KH, HD
    )
    value_rows = jnp.dot(normed_in, full_value, preferred_element_type=jnp.float32).astype(
        jnp.bfloat16
    )
    query_scale = rms_scale(query_raw)
    key_scale = rms_scale(key_raw)
    cos_table, sin_table = rope_tables(where_rows, HD)
    query_rot = rotate(query_raw * query_scale * query_gain, cos_table, sin_table).astype(
        jnp.bfloat16
    )
    key_rot = rotate(key_raw * key_scale * key_gain, cos_table, sin_table).astype(jnp.bfloat16)
    query_heads, key_heads, value_heads = (
        lax.all_to_all(
            query_rot.reshape(seq_count, block_tok, QH * HD),
            "ulysses",
            split_axis=2,
            concat_axis=1,
            tiled=True,
        ),
        lax.all_to_all(
            key_rot.reshape(seq_count, block_tok, KH * HD),
            "ulysses",
            split_axis=2,
            concat_axis=1,
            tiled=True,
        ),
        lax.all_to_all(
            value_rows.reshape(seq_count, block_tok, KH * HD),
            "ulysses",
            split_axis=2,
            concat_axis=1,
            tiled=True,
        ),
    )
    key_all, value_all = (
        lax.all_gather(key_heads, "blk", axis=1, tiled=True),
        lax.all_gather(value_heads, "blk", axis=1, tiled=True),
    )
    attended_list = []
    log_list = []
    for seq_pos in range(seq_count):
        attended_one, log_one = attend(
            query_heads[seq_pos].reshape(group_rows, local_kv, group_size, HD),
            key_all[seq_pos].reshape(-1, local_kv, HD),
            value_all[seq_pos].reshape(-1, local_kv, HD),
            group_where[seq_pos],
            positions[seq_pos],
        )
        attended_list.append(attended_one)
        log_list.append(log_one)
    attended_rows = lax.all_to_all(
        jnp.stack(attended_list), "ulysses", split_axis=1, concat_axis=2, tiled=True
    ).reshape(local_rows, QH * HD)
    middle = tokens_float + jnp.dot(attended_rows, full_out, preferred_element_type=jnp.float32)
    scale_mid = rms_scale(middle)
    normed_mid = (middle * scale_mid * gain_mid).astype(jnp.bfloat16)
    cot_rows = cotangent.reshape(local_rows, model_width)
    part_gate, part_up, part_down = (
        lax.all_gather(w_gate, ("dp", "blk"), axis=1, tiled=True),
        lax.all_gather(w_up, ("dp", "blk"), axis=1, tiled=True),
        lax.all_gather(w_down, ("dp", "blk"), axis=0, tiled=True),
    )
    ffn_in, ffn_cot = (
        lax.all_gather(normed_mid, "ulysses", axis=0, tiled=True),
        lax.all_gather(cot_rows, "ulysses", axis=0, tiled=True),
    )
    gate_pre, up_pre, gate_sigmoid, hidden = ffn_forward(ffn_in, part_gate, part_up)

    def down_rows(start_row, row_count):
        return jnp.dot(hidden, part_down, preferred_element_type=jnp.float32)

    ffn_out = sum_over_group(down_rows, local_rows)
    grad_gate, grad_upward = ffn_backward(
        jnp.dot(ffn_cot, part_down.T, preferred_element_type=jnp.float32),
        gate_pre,
        up_pre,
        gate_sigmoid,
    )

    def back_rows(start_row, row_count):
        return jnp.dot(grad_gate, part_gate.T, preferred_element_type=jnp.float32) + jnp.dot(
            grad_upward, part_up.T, preferred_element_type=jnp.float32
        )

    grad_normed_mid = sum_over_group(back_rows, local_rows)
    grad_w_gate, grad_w_up, grad_w_down = (
        lax.psum_scatter(
            jnp.dot(ffn_in.T, grad_gate, preferred_element_type=jnp.float32).astype(jnp.bfloat16),
            ("dp", "blk"),
            scatter_dimension=1,
            tiled=True,
        ).astype(jnp.float32),
        lax.psum_scatter(
            jnp.dot(ffn_in.T, grad_upward, preferred_element_type=jnp.float32).astype(jnp.bfloat16),
            ("dp", "blk"),
            scatter_dimension=1,
            tiled=True,
        ).astype(jnp.float32),
        lax.psum_scatter(
            jnp.dot(hidden.T, ffn_cot, preferred_element_type=jnp.float32).astype(jnp.bfloat16),
            ("dp", "blk"),
            scatter_dimension=0,
            tiled=True,
        ).astype(jnp.float32),
    )
    block_output = (
        (middle + ffn_out).astype(jnp.bfloat16).reshape(seq_count, block_tok, model_width)
    )
    grad_mid_norm, grad_gain_mid = rms_back(middle, scale_mid, gain_mid, grad_normed_mid, 0)
    grad_middle = cot_rows.astype(jnp.float32) + grad_mid_norm
    grad_middle_low = grad_middle.astype(jnp.bfloat16)
    kept_weights = lax.optimization_barrier(
        (norm_gains, head_gains, w_query, w_key, w_value, w_out, grad_middle_low)
    )
    full_query, full_key, full_value, full_out, full_gains, full_heads = fetch_attention(
        kept_weights[0],
        kept_weights[1],
        kept_weights[2],
        kept_weights[3],
        kept_weights[4],
        kept_weights[5],
    )
    grad_w_out = jnp.dot(attended_rows.T, grad_middle_low, preferred_element_type=jnp.float32)
    grad_attended = jnp.dot(grad_middle_low, full_out.T, preferred_element_type=jnp.float32).astype(
        jnp.bfloat16
    )
    grad_heads = lax.all_to_all(
        grad_attended.reshape(seq_count, block_tok, QH * HD),
        "ulysses",
        split_axis=2,
        concat_axis=1,
        tiled=True,
    )
    query_grads = []
    key_grads = []
    value_grads = []
    for seq_pos in range(seq_count):
        query_grad, key_grad, value_grad = attend_back(
            query_heads[seq_pos].reshape(group_rows, local_kv, group_size, HD),
            key_all[seq_pos].reshape(-1, local_kv, HD),
            value_all[seq_pos].reshape(-1, local_kv, HD),
            group_where[seq_pos],
            positions[seq_pos],
            attended_list[seq_pos],
            log_list[seq_pos],
            grad_heads[seq_pos],
        )
        query_grads.append(query_grad)
        key_grads.append(key_grad)
        value_grads.append(value_grad)
    key_mine, value_mine = (
        lax.psum_scatter(
            jnp.stack(key_grads).astype(jnp.bfloat16), "blk", scatter_dimension=1, tiled=True
        ).astype(jnp.float32),
        lax.psum_scatter(
            jnp.stack(value_grads).astype(jnp.bfloat16), "blk", scatter_dimension=1, tiled=True
        ).astype(jnp.float32),
    )
    query_back, key_back, value_back = (
        lax.all_to_all(
            jnp.stack(query_grads).astype(jnp.bfloat16),
            "ulysses",
            split_axis=1,
            concat_axis=2,
            tiled=True,
        ),
        lax.all_to_all(
            key_mine.astype(jnp.bfloat16), "ulysses", split_axis=1, concat_axis=2, tiled=True
        ),
        lax.all_to_all(
            value_mine.astype(jnp.bfloat16), "ulysses", split_axis=1, concat_axis=2, tiled=True
        ),
    )
    query_pre, grad_query_gain = rms_back(
        query_raw,
        query_scale,
        query_gain,
        unrotate(query_back.reshape(local_rows, QH, HD).astype(jnp.float32), cos_table, sin_table),
        (0, 1),
    )
    key_pre, grad_key_gain = rms_back(
        key_raw,
        key_scale,
        key_gain,
        unrotate(key_back.reshape(local_rows, KH, HD).astype(jnp.float32), cos_table, sin_table),
        (0, 1),
    )
    query_pre_low = query_pre.reshape(local_rows, QH * HD).astype(jnp.bfloat16)
    key_pre_low = key_pre.reshape(local_rows, KH * HD).astype(jnp.bfloat16)
    value_low = value_back.reshape(local_rows, KH * HD)
    grad_w_query = jnp.dot(normed_in.T, query_pre_low, preferred_element_type=jnp.float32)
    grad_w_key = jnp.dot(normed_in.T, key_pre_low, preferred_element_type=jnp.float32)
    grad_w_value = jnp.dot(normed_in.T, value_low, preferred_element_type=jnp.float32)
    grad_normed_in = (
        jnp.dot(query_pre_low, full_query.T, preferred_element_type=jnp.float32)
        + jnp.dot(key_pre_low, full_key.T, preferred_element_type=jnp.float32)
        + jnp.dot(value_low, full_value.T, preferred_element_type=jnp.float32)
    )
    grad_in_norm, grad_gain_in = rms_back(tokens_float, scale_in, gain_in, grad_normed_in, 0)
    grad_input = (grad_middle + grad_in_norm).reshape(seq_count, block_tok, model_width)
    shares = (
        lax.psum_scatter(grad_w_query, ("dp", "blk", "ulysses"), scatter_dimension=0, tiled=True),
        lax.psum_scatter(grad_w_key, ("dp", "blk", "ulysses"), scatter_dimension=0, tiled=True),
        lax.psum_scatter(grad_w_value, ("dp", "blk", "ulysses"), scatter_dimension=0, tiled=True),
        lax.psum_scatter(grad_w_out, ("dp", "blk", "ulysses"), scatter_dimension=0, tiled=True),
        lax.psum_scatter(
            jnp.stack([grad_gain_in, grad_gain_mid]),
            ("dp", "blk", "ulysses"),
            scatter_dimension=1,
            tiled=True,
        ),
        lax.psum_scatter(
            jnp.concatenate([grad_query_gain, grad_key_gain]),
            ("dp", "blk", "ulysses"),
            scatter_dimension=0,
            tiled=True,
        ),
    )
    return (
        block_output,
        grad_input,
        shares[4],
        shares[5],
        shares[0],
        shares[1],
        shares[2],
        shares[3],
        grad_w_gate,
        grad_w_up,
        grad_w_down,
    )


def shift_pairs(size, step):
    return [(source, (source + step) % size) for source in range(size)]


def ring_fetch(shard, axis_name):
    size = lax.axis_size(axis_name)
    return [shard] + [
        lax.ppermute(shard, axis_name, shift_pairs(size, step)) for step in range(1, size)
    ]


def ring_order(pieces, axis_name):
    size = lax.axis_size(axis_name)
    me = lax.axis_index(axis_name)
    ordered = jnp.zeros((size,) + pieces[0].shape, pieces[0].dtype)
    for step, piece in enumerate(pieces):
        ordered = lax.dynamic_update_index_in_dim(ordered, piece, (me - step) % size, 0)
    return ordered


def ring_deliver(pieces, axis_name):
    size = lax.axis_size(axis_name)
    total = pieces[0].astype(jnp.float32)
    moved = [
        lax.ppermute(pieces[step], axis_name, shift_pairs(size, -step)) for step in range(1, size)
    ]
    for piece in moved:
        total = total + piece.astype(jnp.float32)
    return total


def ring_pick(stacked, axis_name):
    size = lax.axis_size(axis_name)
    me = lax.axis_index(axis_name)
    return [
        lax.dynamic_index_in_dim(stacked, (me - step) % size, 0, False) for step in range(size)
    ]


def after(value, *earlier):
    return lax.optimization_barrier((value,) + earlier)[0]


def head_split(values, plane):
    return jnp.moveaxis(values.reshape(values.shape[0], plane, -1), 1, 0)


def plane_device(
    block_input,
    positions,
    cotangent,
    norm_gains,
    head_gains,
    w_query,
    w_key,
    w_value,
    w_out,
    w_gate,
    w_up,
    w_down,
):
    seq_count, block_tok, model_width = block_input.shape
    plane = lax.axis_size("blk") * lax.axis_size("ulysses")
    ring = lax.axis_size("dp")
    my_place = lax.axis_index("blk") * lax.axis_size("ulysses") + lax.axis_index("ulysses")
    local_rows = seq_count * block_tok
    all_rows = plane * local_rows
    seq_len = plane * block_tok
    my_kv = KH // plane
    group_size = QH // KH
    my_q = my_kv * group_size
    weight_rows = w_query.shape[0]
    gain_count = norm_gains.shape[1]
    head_count = head_gains.shape[0]
    q_cols = my_q * HD
    kv_cols = my_kv * HD
    my_cols = q_cols + 2 * kv_cols
    inv_root = 1.0 / math.sqrt(HD)

    gain_row = jnp.concatenate([norm_gains[0], norm_gains[1], head_gains])
    gain_rows = jnp.pad(gain_row[None, :], ((0, 7), (0, my_cols - gain_row.shape[0])))
    packed = jnp.concatenate(
        [
            jnp.concatenate(
                [head_split(w_query, plane), head_split(w_key, plane), head_split(w_value, plane)],
                axis=2,
            ),
            jnp.broadcast_to(gain_rows[None], (plane, 8, my_cols)),
        ],
        axis=1,
    )
    packed = lax.all_to_all(packed, PLANE, split_axis=0, concat_axis=0, tiled=True)
    packed_all = ring_order(ring_fetch(packed, "dp"), "dp")
    out_pieces = ring_fetch(after(w_out, packed), "dp")

    inner = lax.all_gather(
        jnp.stack(
            [
                block_input.reshape(local_rows, model_width),
                cotangent.reshape(local_rows, model_width),
            ]
        ),
        PLANE,
        axis=0,
    )
    tokens_all = inner[:, 0].reshape(all_rows, model_width)
    cot_all = inner[:, 1].reshape(all_rows, model_width)

    out_ordered = ring_order(out_pieces, "dp")
    full_out = lax.all_gather(out_ordered, PLANE, axis=0)
    full_out = jnp.moveaxis(full_out, 0, 1).reshape(QH * HD, model_width)

    gate_t, up_t, _ = lax.optimization_barrier((w_gate.T, w_up.T, packed_all))
    gate_pieces = ring_fetch(gate_t, "dp")
    up_pieces = ring_fetch(up_t, "dp")
    down_pieces = ring_fetch(after(w_down, out_ordered), "dp")
    unit_rows = gate_t.shape[0]

    gains_all = packed_all[:, :, weight_rows, :]
    gain_in = gains_all[..., :gain_count].reshape(-1).astype(jnp.float32)
    gain_mid = gains_all[..., gain_count : 2 * gain_count].reshape(-1).astype(jnp.float32)
    heads_all = (
        gains_all[..., 2 * gain_count : 2 * gain_count + head_count]
        .reshape(-1)
        .astype(jnp.float32)
    )
    query_gain = heads_all[:HD]
    key_gain = heads_all[HD:]
    qkv_weight = packed_all[:, :, :weight_rows, :].reshape(model_width, my_cols)

    tokens_float = tokens_all.astype(jnp.float32)
    scale_in = rms_scale(tokens_float)
    normed_in = (tokens_float * scale_in * gain_in).astype(jnp.bfloat16)
    qkv = jnp.dot(normed_in, qkv_weight, preferred_element_type=jnp.float32)
    where_rows = (
        positions.reshape(seq_count, plane, block_tok).transpose(1, 0, 2).reshape(all_rows)
    )
    cos_table, sin_table = rope_tables(where_rows, HD)
    query_raw = qkv[:, :q_cols].reshape(all_rows, my_q, HD)
    key_raw = qkv[:, q_cols : q_cols + kv_cols].reshape(all_rows, my_kv, HD)
    value_rows = qkv[:, q_cols + kv_cols :].astype(jnp.bfloat16)
    query_scale = rms_scale(query_raw)
    key_scale = rms_scale(key_raw)
    query_rot = rotate(query_raw * query_scale * query_gain, cos_table, sin_table).astype(
        jnp.bfloat16
    )
    key_rot = rotate(key_raw * key_scale * key_gain, cos_table, sin_table).astype(jnp.bfloat16)

    def to_sequences(rows, heads):
        shaped = rows.reshape(plane, seq_count, block_tok, heads, HD)
        return shaped.transpose(1, 3, 0, 2, 4).reshape(seq_count, heads, seq_len, HD)

    def to_rows(values):
        heads = values.shape[1]
        shaped = values.reshape(seq_count, heads, plane, block_tok, HD)
        return shaped.transpose(2, 0, 3, 1, 4).reshape(all_rows, heads * HD)

    queries = to_sequences(query_rot, my_q).reshape(seq_count, my_kv, group_size, seq_len, HD)
    keys = to_sequences(key_rot, my_kv)
    values = to_sequences(value_rows, my_kv)
    allowed = (positions[:, None, :] <= positions[:, :, None])[:, None, None]
    scores = (
        jnp.einsum("skgqd,sktd->skgqt", queries, keys, preferred_element_type=jnp.float32)
        * inv_root
    )
    powers = jnp.where(allowed, jnp.exp(scores), 0.0)
    shares = powers * (1.0 / jnp.sum(powers, axis=-1, keepdims=True))
    weights = shares.astype(jnp.bfloat16)
    attended = jnp.einsum(
        "skgqt,sktd->skgqd", weights, values, preferred_element_type=jnp.float32
    ).astype(jnp.bfloat16)
    attended_mine = to_rows(attended.reshape(seq_count, my_q, seq_len, HD))
    attended_all = lax.all_gather(attended_mine, PLANE, axis=1, tiled=True)

    middle = tokens_float + jnp.dot(attended_all, full_out, preferred_element_type=jnp.float32)
    scale_mid = rms_scale(middle)
    unit_mid = middle * scale_mid
    normed_mid = (unit_mid * gain_mid).astype(jnp.bfloat16)

    gate_up = jnp.concatenate(gate_pieces + up_pieces, axis=0)
    units = ring * unit_rows
    down = jnp.concatenate(down_pieces, axis=0)
    gate_up_pre = lax.dot_general(
        normed_mid, gate_up, (((1,), (1,)), ((), ())), preferred_element_type=jnp.float32
    )
    gate_pre = gate_up_pre[:, :units]
    up_pre = gate_up_pre[:, units:]
    grad_hidden = lax.dot_general(
        cot_all, down, (((1,), (1,)), ((), ())), preferred_element_type=jnp.float32
    )
    gate_sigmoid = jax.nn.sigmoid(gate_pre)
    hidden = (gate_pre * gate_sigmoid * up_pre).astype(jnp.bfloat16)
    grad_gate, grad_upward = ffn_backward(grad_hidden, gate_pre, up_pre, gate_sigmoid)
    grad_pair = jnp.concatenate([grad_gate, grad_upward], axis=1)
    back_part = jnp.dot(grad_pair, gate_up, preferred_element_type=jnp.float32)
    gain_mid_part = jnp.sum(back_part * unit_mid, axis=0)
    grad_normed_mid = lax.psum_scatter(
        back_part.astype(jnp.bfloat16), PLANE, scatter_dimension=0, tiled=True
    ).astype(jnp.float32)

    grad_gate_up = lax.dot_general(
        grad_pair, normed_mid, (((0,), (0,)), ((), ())), preferred_element_type=jnp.float32
    ).astype(jnp.bfloat16)
    grad_down = lax.dot_general(
        hidden, cot_all, (((0,), (0,)), ((), ())), preferred_element_type=jnp.float32
    ).astype(jnp.bfloat16)
    unit_chunks = [grad_gate_up[step * unit_rows : (step + 1) * unit_rows] for step in range(2 * ring)]
    grad_w_gate = ring_deliver(unit_chunks[:ring], "dp").T
    grad_w_up = ring_deliver(unit_chunks[ring:], "dp").T
    grad_w_down = ring_deliver(
        [grad_down[step * unit_rows : (step + 1) * unit_rows] for step in range(ring)], "dp"
    )

    my_middle = lax.dynamic_slice_in_dim(middle, my_place * local_rows, local_rows, 0)
    my_scale = lax.dynamic_slice_in_dim(scale_mid, my_place * local_rows, local_rows, 0)
    grad_mid_norm, _ = rms_back(my_middle, my_scale, gain_mid, grad_normed_mid, 0)
    grad_middle = cotangent.reshape(local_rows, model_width).astype(jnp.float32) + grad_mid_norm
    grad_low_all = lax.all_gather(grad_middle.astype(jnp.bfloat16), PLANE, axis=0, tiled=True)

    out_part = jnp.dot(hidden, down, preferred_element_type=jnp.float32).astype(jnp.bfloat16)
    ffn_out = lax.psum_scatter(
        after(out_part, grad_low_all), PLANE, scatter_dimension=0, tiled=True
    ).astype(jnp.float32)
    block_output = (my_middle + ffn_out).astype(jnp.bfloat16).reshape(block_input.shape)

    my_out = lax.dynamic_slice_in_dim(full_out, my_place * q_cols, q_cols, 0)
    grad_attended = lax.dot_general(
        grad_low_all, my_out, (((1,), (1,)), ((), ())), preferred_element_type=jnp.float32
    ).astype(jnp.bfloat16)
    owned_attended = lax.dynamic_index_in_dim(
        attended_all.reshape(all_rows, ring, plane, weight_rows), my_place, 2, False
    ).reshape(all_rows, ring * weight_rows)
    grad_out = (
        lax.dot_general(
            owned_attended, grad_low_all, (((0,), (0,)), ((), ())), preferred_element_type=jnp.float32
        )
        .astype(jnp.bfloat16)
        .reshape(ring, weight_rows, model_width)
    )
    grad_w_out = ring_deliver(ring_pick(grad_out, "dp"), "dp")

    grad_heads = to_sequences(grad_attended, my_q).reshape(queries.shape)
    deltas = jnp.sum(
        grad_heads.astype(jnp.float32) * attended.astype(jnp.float32), axis=-1, keepdims=True
    )
    grad_weights = jnp.einsum(
        "skgqd,sktd->skgqt", grad_heads, values, preferred_element_type=jnp.float32
    )
    grad_scores = (shares * (grad_weights - deltas)).astype(jnp.bfloat16)
    query_grad = (
        jnp.einsum("skgqt,sktd->skgqd", grad_scores, keys, preferred_element_type=jnp.float32)
        * inv_root
    ).astype(jnp.bfloat16)
    key_grad = (
        jnp.einsum("skgqt,skgqd->sktd", grad_scores, queries, preferred_element_type=jnp.float32)
        * inv_root
    ).astype(jnp.bfloat16)
    value_grad = jnp.einsum(
        "skgqt,skgqd->sktd", weights, grad_heads, preferred_element_type=jnp.float32
    ).astype(jnp.bfloat16)
    query_back = to_rows(query_grad.reshape(seq_count, my_q, seq_len, HD))
    query_pre, grad_query_gain = rms_back(
        query_raw,
        query_scale,
        query_gain,
        unrotate(query_back.reshape(all_rows, my_q, HD).astype(jnp.float32), cos_table, sin_table),
        (0, 1),
    )
    key_pre, grad_key_gain = rms_back(
        key_raw,
        key_scale,
        key_gain,
        unrotate(
            to_rows(key_grad).reshape(all_rows, my_kv, HD).astype(jnp.float32), cos_table, sin_table
        ),
        (0, 1),
    )
    grad_qkv = jnp.concatenate(
        [
            query_pre.reshape(all_rows, q_cols).astype(jnp.bfloat16),
            key_pre.reshape(all_rows, kv_cols).astype(jnp.bfloat16),
            to_rows(value_grad),
        ],
        axis=1,
    )
    in_part = lax.dot_general(
        grad_qkv, qkv_weight, (((1,), (1,)), ((), ())), preferred_element_type=jnp.float32
    )
    gain_in_part = jnp.sum(in_part * (tokens_float * scale_in), axis=0)
    grad_normed_in = lax.psum_scatter(
        in_part.astype(jnp.bfloat16), PLANE, scatter_dimension=0, tiled=True
    ).astype(jnp.float32)
    grad_qkv_weight = lax.dot_general(
        normed_in, grad_qkv, (((0,), (0,)), ((), ())), preferred_element_type=jnp.float32
    ).astype(jnp.bfloat16)
    gain_parts = jnp.concatenate(
        [
            gain_in_part.reshape(ring, plane, gain_count),
            gain_mid_part.reshape(ring, plane, gain_count),
            jnp.concatenate([grad_query_gain, grad_key_gain]).reshape(ring, plane, head_count),
        ],
        axis=2,
    ).astype(jnp.bfloat16)
    gain_parts = jnp.pad(
        gain_parts[:, :, None, :], ((0, 0), (0, 0), (0, 7), (0, my_cols - gain_parts.shape[2]))
    )
    grad_packed = jnp.concatenate(
        [grad_qkv_weight.reshape(ring, plane, weight_rows, my_cols), gain_parts], axis=2
    )
    grad_packed = ring_deliver(ring_pick(grad_packed, "dp"), "dp").astype(jnp.bfloat16)
    grad_packed = lax.all_to_all(grad_packed, PLANE, split_axis=0, concat_axis=0, tiled=True)
    owned = jnp.moveaxis(grad_packed[:, :weight_rows], 0, 1).astype(jnp.float32)
    grad_w_query = owned[:, :, :q_cols].reshape(weight_rows, QH * HD)
    grad_w_key = owned[:, :, q_cols : q_cols + kv_cols].reshape(weight_rows, KH * HD)
    grad_w_value = owned[:, :, q_cols + kv_cols :].reshape(weight_rows, KH * HD)
    gain_sums = jnp.sum(grad_packed[:, weight_rows].astype(jnp.float32), axis=0)
    grad_norm_gains = gain_sums[: 2 * gain_count].reshape(2, gain_count)
    grad_head_gains = gain_sums[2 * gain_count : 2 * gain_count + head_count]

    my_tokens = block_input.reshape(local_rows, model_width).astype(jnp.float32)
    grad_in_norm, _ = rms_back(my_tokens, rms_scale(my_tokens), gain_in, grad_normed_in, 0)
    grad_input = (grad_middle + grad_in_norm).reshape(block_input.shape)
    return (
        block_output,
        grad_input,
        grad_norm_gains,
        grad_head_gains,
        grad_w_query,
        grad_w_key,
        grad_w_value,
        grad_w_out,
        grad_w_gate,
        grad_w_up,
        grad_w_down,
    )


def solution(mesh):
    plane = mesh.shape["blk"] * mesh.shape["ulysses"]
    heads_fit = KH % plane == 0
    return jax.shard_map(
        plane_device if heads_fit else per_device,
        mesh=mesh,
        in_specs=(
            P("dp", ("blk", "ulysses"), None),
            P("dp", None),
            P("dp", ("blk", "ulysses"), None),
            P(None, ("dp", "blk", "ulysses")),
            P(("dp", "blk", "ulysses")),
            P(("dp", "blk", "ulysses"), None),
            P(("dp", "blk", "ulysses"), None),
            P(("dp", "blk", "ulysses"), None),
            P(("dp", "blk", "ulysses"), None),
            P(None, ("dp", "blk", "ulysses")),
            P(None, ("dp", "blk", "ulysses")),
            P(("dp", "blk", "ulysses"), None),
        ),
        out_specs=(
            P("dp", ("blk", "ulysses"), None),
            P("dp", ("blk", "ulysses"), None),
            P(None, ("dp", "blk", "ulysses")),
            P(("dp", "blk", "ulysses")),
            P(("dp", "blk", "ulysses"), None),
            P(("dp", "blk", "ulysses"), None),
            P(("dp", "blk", "ulysses"), None),
            P(("dp", "blk", "ulysses"), None),
            P(None, ("dp", "blk", "ulysses")),
            P(None, ("dp", "blk", "ulysses")),
            P(("dp", "blk", "ulysses"), None),
        ),
        check_vma=False,
    )
```
